256 devices in a mesh: dp: 64 (over x, z, core), tensor: 4 (over y).
Axes of the slice: x: 4, y: 4, z: 8, core: 2. Of those that a mesh axis runs over, the one named last changes fastest.
Arguments:
- gate_preactivation: bfloat16 [1024, 28672], P('dp', 'tensor'), may hold values from -6 to 6
- up_preactivation: bfloat16 [1024, 28672], P('dp', 'tensor'), may hold values from -6 to 6
- cotangent: bfloat16 [1024, 8192], P('dp'), may hold values from -0.1875 to 0.1875
- down_weight: bfloat16 [28672, 8192], P('tensor', 'dp'), may hold values from -0.03125 to 0.03125
- lowrank_factor_first: bfloat16 [28672, 64], P('tensor'), may hold values from -0.03125 to 0.03125
- lowrank_factor_second: bfloat16 [64, 8192], replicated, may hold values from -0.75 to 0.75
- sparse_block_values: bfloat16 [64, 4, 2, 128, 128], P('dp', 'tensor'), may hold values from -0.5 to 0.5
- slot_block_rows: int32 [64, 4, 2], P(None, 'tensor'), may hold values from 0 to 55, as said below
- slot_block_columns: int32 [64, 4, 2], P(None, 'tensor'), may hold values from 0 to 0
- owner_slot_counts: int32 [64, 4], P(None, 'tensor'), may hold values from 1 to 2, as said below
Outputs:
- mixed: bfloat16 [1024, 8192], P('tensor', 'dp')
- grad_a: float32 [28672, 64], P('tensor')
- grad_b: float32 [64, 8192], P(None, 'dp')
- grad_blocks: float32 [64, 4, 2, 128, 128], P('dp', 'tensor')
The draws below stay inside these ranges and needn't reach their ends.
Inputs may be any that keep to these rules, and one draw needn't show every extreme that they name: `slot_block_rows`: the 2 slots of one owner name different blocks. `owner_slot_counts`: some owner has exactly 2 live slots.
All inputs are finite; a program needn't handle non-finite values.
Results may differ from the reference program's by a relative error of at most 0.0049.
Values may be sent and summed in bfloat16 or wider, within the bound.
No kernel may reach another device: no remote copies, remote signals or barrier semaphores. Data moves between devices by JAX's collectives and lax.ppermute only.
A program may use at most 128 MiB of HBM per device.

```python
import jax
import jax.numpy as jnp
from jax import lax

MODEL_WIDTH = 8192
HIDDEN_UNITS = 28672
ADAPTER_RANK = 64
BS = 128
CAP = 2
TOKENS = 1024
N_DP = 64
N_TENSOR = 4


def block_choice(key):
    inner = jax.random.fold_in(key, 11)
    spots = HIDDEN_UNITS // N_TENSOR // BS * (MODEL_WIDTH // N_DP // BS)
    scores = jax.random.randint(inner, (N_DP, N_TENSOR, spots), 0, 1 << 20) * spots + jnp.arange(spots, dtype=jnp.int32)
    return jnp.argsort(scores, axis=-1)[..., :CAP].astype(jnp.int32)


def draw_slot_block_rows(key, part):
    return (block_choice(key) // (MODEL_WIDTH // N_DP // BS)).astype(jnp.int32)


def draw_slot_block_columns(key, part):
    return (block_choice(key) % (MODEL_WIDTH // N_DP // BS)).astype(jnp.int32)


def draw_owner_slot_counts(key, part):
    counts = jax.random.randint(jax.random.fold_in(key, 23), (N_DP * N_TENSOR,), 1, CAP + 1)
    spot = jax.random.randint(jax.random.fold_in(key, 29), (), 0, N_DP * N_TENSOR)
    counts = jnp.where(jnp.arange(N_DP * N_TENSOR, dtype=jnp.int32) == spot, CAP, counts)
    return counts.reshape(N_DP, N_TENSOR).astype(jnp.int32)


def block_levels(own_key, shape, shards, low, top_value):
    level = 1.0
    for axis_at, blocks in shards:
        steps = jax.random.uniform(jax.random.fold_in(jax.random.fold_in(own_key, 6), axis_at), (blocks,), jnp.float32, low / len(shards), top_value / len(shards))
        level = level * jnp.repeat(jnp.exp(steps), shape[axis_at] // blocks).reshape((-1,) + (1,) * (len(shape) - 1 - axis_at))
    return level


def bell_draw(stream_key, shape, scale, reach, pieces=(), kind=jnp.bfloat16):
    loudness = block_levels(stream_key, shape, pieces, -0.22, 0.18) if pieces else 1.0
    drawn = jax.random.normal(stream_key, shape, jnp.float32) * scale * loudness
    return jnp.minimum(jnp.maximum(drawn, -reach), reach).astype(kind)


def setup_inputs(seed: int = 0) -> dict:
    seeds = jax.random.split(jax.random.key(seed), 11)
    return {
        "gate_preactivation": bell_draw(seeds[0], (TOKENS, HIDDEN_UNITS), 1.0, 6.0, ((0, 64), (1, 4))),
        "up_preactivation": bell_draw(seeds[1], (TOKENS, HIDDEN_UNITS), 1.0, 6.0, ((0, 64), (1, 4))),
        "cotangent": bell_draw(seeds[2], (TOKENS, MODEL_WIDTH), (TOKENS ** -0.5), 0.1875, ((0, 64),)),
        "down_weight": bell_draw(seeds[3], (HIDDEN_UNITS, MODEL_WIDTH), HIDDEN_UNITS ** -0.5, 0.03125, ((0, 4), (1, 64))),
        "lowrank_factor_first": bell_draw(seeds[4], (HIDDEN_UNITS, ADAPTER_RANK), HIDDEN_UNITS ** -0.5, 0.03125, ((0, 4),)),
        "lowrank_factor_second": bell_draw(seeds[5], (ADAPTER_RANK, MODEL_WIDTH), ADAPTER_RANK ** -0.5, 0.75),
        "sparse_block_values": bell_draw(seeds[6], (N_DP, N_TENSOR, CAP, BS, BS), BS ** -0.5, 0.5, ((0, 64), (1, 4))),
        "slot_block_rows": draw_slot_block_rows(jax.random.fold_in(seeds[10], 71), 0),
        "slot_block_columns": draw_slot_block_columns(jax.random.fold_in(seeds[10], 71), 0),
        "owner_slot_counts": draw_owner_slot_counts(jax.random.fold_in(seeds[10], 71), 0),
    }


def reference(gate_preactivation, up_preactivation, cotangent, down_weight, lowrank_factor_first, lowrank_factor_second, sparse_block_values, slot_block_rows, slot_block_columns, owner_slot_counts):
    hidden_activation = (jax.nn.silu(gate_preactivation.astype(jnp.float32)) * up_preactivation.astype(jnp.float32)).astype(jnp.bfloat16)
    lowrank_projection = jnp.dot(hidden_activation, lowrank_factor_first, preferred_element_type=jnp.float32)
    frozen_product = jnp.dot(hidden_activation, down_weight, preferred_element_type=jnp.float32)
    frozen_product = frozen_product + jnp.dot(lowrank_projection, lowrank_factor_second.astype(jnp.float32), precision=lax.Precision.HIGHEST)
    per_row = HIDDEN_UNITS // N_TENSOR // BS
    per_col = MODEL_WIDTH // N_DP // BS
    live = (jnp.arange(CAP, dtype=jnp.int32)[None, None, :] < owner_slot_counts[:, :, None]).astype(jnp.float32)
    global_rows = (jnp.arange(N_TENSOR, dtype=jnp.int32)[None, :, None] * per_row + slot_block_rows).astype(jnp.int32)
    picked = jnp.take(hidden_activation.reshape(TOKENS, HIDDEN_UNITS // BS, BS), global_rows.reshape(-1), axis=1)
    picked = picked.reshape(TOKENS, N_DP, N_TENSOR, CAP, BS).astype(jnp.float32)
    local = jnp.einsum("tojkc,ojkcd->tojkd", picked, sparse_block_values.astype(jnp.float32), precision=lax.Precision.HIGHEST)
    col_pick = (slot_block_columns[..., None] == jnp.arange(per_col, dtype=jnp.int32)).astype(jnp.float32)
    spread = jnp.einsum("tojkd,ojkn->tond", local, col_pick * live[..., None], precision=lax.Precision.HIGHEST)
    mixed = (frozen_product + spread.reshape(TOKENS, MODEL_WIDTH)).astype(jnp.bfloat16)
    cotangent_lowrank = lax.dot_general(cotangent, lowrank_factor_second, (((1,), (1,)), ((), ())), preferred_element_type=jnp.float32).astype(jnp.bfloat16)
    grad_a = lax.dot_general(hidden_activation, cotangent_lowrank, (((0,), (0,)), ((), ())), preferred_element_type=jnp.float32)
    grad_b = lax.dot_general(lowrank_projection, cotangent.astype(jnp.float32), (((0,), (0,)), ((), ())), precision=lax.Precision.HIGHEST)
    cot_cols = cotangent.reshape(TOKENS, N_DP, per_col, BS).astype(jnp.float32)
    cot_pick = jnp.einsum("tond,ojkn->tojkd", cot_cols, col_pick, precision=lax.Precision.HIGHEST)
    grad_blocks = jnp.einsum("tojkc,tojkd->ojkcd", picked, cot_pick, precision=lax.Precision.HIGHEST)
    grad_blocks = grad_blocks * live[..., None, None]
    return (mixed, grad_a, grad_b, grad_blocks)
```

```python
import functools

import jax
import jax.numpy as jnp
from jax import lax
from jax.experimental import pallas as pl
from jax.experimental.pallas import tpu as pltpu
from jax.sharding import Mesh
from jax.sharding import PartitionSpec as P


DP = ("x", "z", "c")
NX, NZ = 4, 8
bf = jnp.bfloat16
f32 = jnp.float32
CA = 3584
BLK = 1792
BIG = 60
XS = (0, -1, 1, 2)
ZS = (0, -1, 1, -2, 2, -3, 3, 4)


def shift(a, axis, k):
    n = lax.axis_size(axis)
    return lax.ppermute(a, axis, [(i, (i + k) % n) for i in range(n)])


def tn(a, b):
    return lax.dot_general(a, b, (((0,), (0,)), ((), ())), preferred_element_type=f32)


def kernel_stack(n, *refs):
    for k in range(n):
        refs[n + k // (n // 2)][k % (n // 2)] = refs[k][...]


def stack(parts):
    vm = pl.BlockSpec(memory_space=pltpu.VMEM)
    n = len(parts)
    half = jax.ShapeDtypeStruct((n // 2, *parts[0].shape), parts[0].dtype)
    return pl.pallas_call(
        functools.partial(kernel_stack, n),
        in_specs=[vm] * n,
        out_specs=[vm] * 2,
        out_shape=[half] * 2,
        compiler_params=params(8),
        name="stack",
    )(*parts)


def kernel_prep(s_ref, w_ref, wo_ref, at_ref, b_ref, sp_ref, spo_ref, out_ref):
    i = pl.program_id(0)
    own = s_ref[2]
    ab = tn(at_ref[...], b_ref[...])
    rows = out_ref.shape[0]
    for c in range(2):
        cols = slice(c * 128, (c + 1) * 128)

        @pl.when(own == c)
        def _():
            out_ref[:, cols] = (w_ref[...].astype(f32) + ab[:, cols]).astype(bf)

        @pl.when(own != c)
        def _():
            out_ref[:, cols] = (wo_ref[...].astype(f32) + ab[:, cols]).astype(bf)

    for j in range(4):
        at = s_ref[3 + j] * 128 - i * rows

        @pl.when((at >= 0) & (at < rows) & (s_ref[7 + j] > 0))
        def _():
            sp = sp_ref[j] if j < 2 else spo_ref[j - 2]
            c = own if j < 2 else 1 - own
            here = (pl.ds(pl.multiple_of(at, 128), 128), pl.ds(pl.multiple_of(c * 128, 128), 128))
            out_ref[here] = (out_ref[here].astype(f32) + sp.astype(f32)).astype(bf)


def assemble(scr, ref_list, places, xi, zi):
    for ref, place in zip(ref_list, places):
        for k, (dx, dz) in enumerate(place):
            row = (lax.rem(xi + dx + NX, NX) * NZ + lax.rem(zi + dz + NZ, NZ)) * 16
            scr[pl.ds(pl.multiple_of(row, 16), 16), :] = ref[k]


def kernel_a(places, n, s_ref, *refs):
    chunks, ext = refs[:n], refs[n : 2 * n]
    w_ref, cot_ref, out_ref, ga_ref, clt_ref, low_ref, gs_ref, scr, ext_scr = refs[2 * n :]
    i = pl.program_id(0)
    xi, zi = s_ref[0], s_ref[1]

    @pl.when(i == 0)
    def _():
        assemble(ext_scr, ext, places, xi, zi)
        low_ref[...] = ext_scr[...]
        clt_ref[...] = ext_scr[...].astype(f32).T.astype(bf)
        gs_ref[...] = jnp.zeros_like(gs_ref)

    assemble(scr, chunks, places, xi, zi)
    h = scr[...]
    part = jnp.dot(h, w_ref[...], preferred_element_type=f32)

    @pl.when(i == 0)
    def _():
        out_ref[...] = part

    @pl.when(i > 0)
    def _():
        out_ref[...] += part

    ga_ref[...] = jnp.dot(clt_ref[:64, :], h, preferred_element_type=f32)
    picks(i, 0, s_ref, scr, cot_ref, gs_ref)


def kernel_b(places, n, s_ref, *refs):
    chunks = refs[:n]
    w_ref, cot_ref, outa_ref, clt_ref, low_ref, gsa_ref, send_ref, ga_ref, gs_ref, scr, acc = refs[n:]
    i = pl.program_id(0)
    xi, zi = s_ref[0], s_ref[1]
    assemble(scr, chunks, places, xi, zi)
    h = scr[...]
    part = jnp.dot(h, w_ref[...], preferred_element_type=f32)

    @pl.when(i == 0)
    def _():
        acc[...] = outa_ref[...] + part
        gs_ref[...] = gsa_ref[...]

    @pl.when(i == pl.num_programs(0) - 1)
    def _():
        out = acc[...] + part
        gb = tn(low_ref[...], cot_ref[...])[64:]
        for c in range(2):
            for y in range(4):
                send_ref[c * 4 + y, :128, :] = out[y * 128 : (y + 1) * 128, c * 128 : (c + 1) * 128]
                send_ref[c * 4 + y, 128:, :] = gb[:, c * 128 : (c + 1) * 128]

    ga_ref[...] = jnp.dot(clt_ref[:64, :], h, preferred_element_type=f32)
    picks(i, CA // 128, s_ref, scr, cot_ref, gs_ref)


def picks(i, base, s_ref, scr, cot_ref, gs_ref):
    for j in range(4):
        at = (s_ref[3 + j] - base) * 128 - i * BLK

        @pl.when((at >= 0) & (at < BLK))
        def _():
            c = s_ref[2] if j < 2 else 1 - s_ref[2]
            cot = cot_ref[:, pl.ds(pl.multiple_of(c * 128, 128), 128)]
            gs_ref[j] = tn(scr[:, pl.ds(pl.multiple_of(at, 128), 128)], cot)


def kernel_final(got_ref, mixed_ref, gb_ref):
    acc = None
    for c in range(2):
        s = got_ref[c * 4]
        for y in range(1, 4):
            s = s + got_ref[c * 4 + y]
        for z in range(NZ):
            mixed_ref[z, c] = s[z * 16 : (z + 1) * 16].astype(bf)
        acc = s[128:] if acc is None else acc + s[128:]
    gb_ref[...] = acc


def kernel_add(x_ref, y_ref, o_ref):
    o_ref[...] = x_ref[...] + y_ref[...]


def kernel_add_to(_, x_ref, y_ref, o_ref):
    o_ref[...] = x_ref[...] + y_ref[...]


def params(mib=24):
    return pltpu.CompilerParams(vmem_limit_bytes=mib << 20)


def shards(gate, up, cot, w, a, b, sbv, rows, cols, counts):
    xi, zi, ci = lax.axis_index("x"), lax.axis_index("z"), lax.axis_index("c")
    chip = xi * NZ + zi
    K = w.shape[0]
    CB = K - CA
    first = ci == 0
    hid = (jax.nn.silu(gate.astype(f32)) * up.astype(f32)).astype(bf)
    own_b = hid[:, CA:]
    cl = lax.dot_general(cot, b, (((1,), (1,)), ((), ())), preferred_element_type=f32).astype(bf)
    lo = jnp.dot(hid, a, preferred_element_type=f32).astype(bf)
    own_a = jnp.concatenate([hid[:, :CA], cl, lo], axis=1)
    fb, bb = [own_b], [own_b]
    for _ in range(1, 4):
        fb.append(shift(fb[-1], "z", 1))
        bb.append(shift(bb[-1], "z", -1))
    sb = stack([own_b, fb[1], bb[1], fb[2], bb[2], fb[3], bb[3], shift(fb[3], "z", 1)])
    sa = stack([own_a, shift(own_a, "x", 1), shift(own_a, "x", -1), shift(own_a, "x", 2)])
    chunks_a, places_a = list(sa), [[(x, 0) for x in XS[:2]], [(x, 0) for x in XS[2:]]]
    f, r = list(sa), list(sa)
    for k in range(1, 5):
        for h in (0, 1):
            if k < 4 or h == 0:
                f[h] = shift(f[h], "z", 1)
                chunks_a.append(f[h])
                places_a.append([(x, -k) for x in XS[2 * h : 2 * h + 2]])
        for h in (1, 0):
            if k < 4 or h == 1:
                r[h] = shift(r[h], "z", -1)
                chunks_a.append(r[h])
                places_a.append([(x, k) for x in XS[2 * h : 2 * h + 2]])
    xf = [shift(sb[0], "x", 1), shift(sb[1], "x", 1)]
    xb = [shift(sb[0], "x", -1), shift(sb[1], "x", -1)]
    chunks_b = [*sb, *xf, *xb, shift(xf[0], "x", 1), shift(xb[1], "x", -1)]
    zs = [list(ZS[:4]), list(ZS[4:])]
    places_b = [[(x, z) for z in zs[h]] for x in XS for h in (0, 1)]
    sp = sbv[0, 0]
    w_o = shift(w, "c", 1)
    sp_o = shift(sp, "c", 1)
    b2 = lax.dynamic_slice_in_dim(b, chip * 256, 256, 1)
    r2 = lax.dynamic_slice_in_dim(rows[:, 0, :], chip * 2, 2, 0)
    live = jnp.arange(2, dtype=jnp.int32)[None, :] < lax.dynamic_slice_in_dim(counts[:, 0], chip * 2, 2, 0)[:, None]
    rel = jnp.where(first, r2, r2[::-1])
    rlive = jnp.where(first, live, live[::-1])
    scal = jnp.concatenate(
        [jnp.stack([xi, zi, ci]).astype(jnp.int32), rel.reshape(4), rlive.astype(jnp.int32).reshape(4)]
    )
    cc = lax.all_to_all(cot.reshape(16, 32, 256), ("x", "z"), split_axis=1, concat_axis=0)
    cc = cc.reshape(512, 256)

    def col(shape, off=0):
        return pl.BlockSpec(shape, lambda i, s: (0,) * (len(shape) - 1) + (i + off,))

    def whole(shape, at=None):
        return pl.BlockSpec(shape, lambda i, s: at or (0,) * len(shape))

    na, nb = len(chunks_a), len(chunks_b)
    cost = pl.CostEstimate(flops=2 * 512 * CA * 384, bytes_accessed=12 << 20, transcendentals=0)
    weff = pl.pallas_call(
        kernel_prep,
        grid_spec=pltpu.PrefetchScalarGridSpec(
            num_scalar_prefetch=1,
            grid=(K // BLK,),
            in_specs=[
                pl.BlockSpec((BLK, 128), lambda i, s: (i, 0)),
                pl.BlockSpec((BLK, 128), lambda i, s: (i, 0)),
                col((64, BLK)),
                whole((64, 256)),
                whole((2, 128, 128)),
                whole((2, 128, 128)),
            ],
            out_specs=pl.BlockSpec((BLK, 256), lambda i, s: (i, 0)),
        ),
        out_shape=jax.ShapeDtypeStruct((K, 256), bf),
        compiler_params=params(BIG),
        cost_estimate=pl.CostEstimate(flops=1 << 28, bytes_accessed=8 << 20, transcendentals=0),
        name="prep",
    )(scal, w, w_o, a.T, b2, sp, sp_o)
    out_a, ga_a, clt, low, gs_a = pl.pallas_call(
        functools.partial(kernel_a, places_a, na),
        grid_spec=pltpu.PrefetchScalarGridSpec(
            num_scalar_prefetch=1,
            grid=(CA // BLK,),
            in_specs=[col((x.shape[0], 16, BLK)) for x in chunks_a]
            + [whole((x.shape[0], 16, 128), (0, 0, CA // 128)) for x in chunks_a]
            + [pl.BlockSpec((BLK, 256), lambda i, s: (i, 0)), whole((512, 256))],
            out_specs=[whole((512, 256)), col((64, BLK)), whole((128, 512)), whole((512, 128)), whole((4, 128, 128))],
            scratch_shapes=[pltpu.VMEM((512, BLK), bf), pltpu.VMEM((512, 128), bf)],
        ),
        out_shape=[
            jax.ShapeDtypeStruct((512, 256), f32),
            jax.ShapeDtypeStruct((64, CA), f32),
            jax.ShapeDtypeStruct((128, 512), bf),
            jax.ShapeDtypeStruct((512, 128), bf),
            jax.ShapeDtypeStruct((4, 128, 128), f32),
        ],
        compiler_params=params(BIG),
        cost_estimate=cost,
        name="colour_a",
    )(scal, *chunks_a, *chunks_a, weff, cc)
    send, ga_b, gs = pl.pallas_call(
        functools.partial(kernel_b, places_b, nb),
        grid_spec=pltpu.PrefetchScalarGridSpec(
            num_scalar_prefetch=1,
            grid=(CB // BLK,),
            in_specs=[col((x.shape[0], 16, BLK)) for x in chunks_b]
            + [
                pl.BlockSpec((BLK, 256), lambda i, s: (i + CA // BLK, 0)),
                whole((512, 256)),
                whole((512, 256)),
                whole((128, 512)),
                whole((512, 128)),
                whole((4, 128, 128)),
            ],
            out_specs=[whole((8, 192, 128)), col((64, BLK)), whole((4, 128, 128))],
            scratch_shapes=[pltpu.VMEM((512, BLK), bf), pltpu.VMEM((512, 256), f32)],
        ),
        out_shape=[
            jax.ShapeDtypeStruct((8, 192, 128), f32),
            jax.ShapeDtypeStruct((64, CB), f32),
            jax.ShapeDtypeStruct((4, 128, 128), f32),
        ],
        compiler_params=params(BIG),
        cost_estimate=cost,
        name="colour_b",
    )(scal, *chunks_b, weff, cc, out_a, clt, low, gs_a)
    vm = pl.BlockSpec(memory_space=pltpu.VMEM)
    got = lax.all_to_all(send, ("c", "y"), 0, 0, tiled=True)
    gsum = gs[:2] + shift(gs[2:], "c", 1)
    grad_blocks = jnp.where(rlive[0][:, None, None], gsum, 0.0)[None, None]
    left = pl.BlockSpec((64, BLK), lambda i: (0, i))
    grad_a = pl.pallas_call(
        kernel_add,
        grid=(CA // BLK,),
        in_specs=[left, left],
        out_specs=left,
        out_shape=jax.ShapeDtypeStruct((64, K), f32),
        compiler_params=params(8),
        name="add_a",
    )(ga_a, shift(ga_a, "c", 1))
    grad_a = pl.pallas_call(
        kernel_add_to,
        grid=(CB // BLK,),
        in_specs=[pl.BlockSpec(memory_space=pl.ANY), left, left],
        out_specs=pl.BlockSpec((64, BLK), lambda i: (0, i + CA // BLK)),
        out_shape=jax.ShapeDtypeStruct((64, K), f32),
        input_output_aliases={0: 0},
        compiler_params=params(8),
        name="add_b",
    )(grad_a, ga_b, shift(ga_b, "c", 1)).T
    mixed, grad_b = pl.pallas_call(
        kernel_final,
        in_specs=[vm],
        out_specs=[vm, vm],
        out_shape=[jax.ShapeDtypeStruct((NZ, 2, 16, 128), bf), jax.ShapeDtypeStruct((64, 128), f32)],
        compiler_params=params(),
        name="final",
    )(got)
    return (mixed.reshape(256, 128), grad_a, grad_b, grad_blocks)


def solution(mesh):
    finer = Mesh(mesh.devices.reshape(4, 8, 2, 4), ("x", "z", "c", "y"))
    in_specs = (
        P(DP, "y"),
        P(DP, "y"),
        P(DP, None),
        P("y", DP),
        P("y", None),
        P(),
        P(DP, "y", None, None, None),
        P(None, "y", None),
        P(None, "y", None),
        P(None, "y"),
    )
    out_specs = (P("y", DP), P("y", None), P(None, DP), P(DP, "y", None, None, None))
    return jax.shard_map(shards, mesh=finer, in_specs=in_specs, out_specs=out_specs, check_vma=False)
```

```python
import functools

import jax
import jax.numpy as jnp
from jax import lax
from jax.experimental import pallas as pl
from jax.experimental.pallas import tpu as pltpu
from jax.sharding import Mesh
from jax.sharding import PartitionSpec as P


DP = ("x", "z", "c")
NX, NZ = 4, 8
bf = jnp.bfloat16
f32 = jnp.float32
CA = 3584
BLK = 1792
GRANT = 18
XS = (0, -1, 1, 2)
ZS = (0, -1, 1, -2, 2, -3, 3, 4)


def shift(a, axis, k):
    n = lax.axis_size(axis)
    return lax.ppermute(a, axis, [(i, (i + k) % n) for i in range(n)])


def tn(a, b):
    return lax.dot_general(a, b, (((0,), (0,)), ((), ())), preferred_element_type=f32)


def kernel_stack(n, per, *refs):
    for k in range(n):
        refs[n + k // per][k % per] = refs[k][...]


def stack(parts, halves):
    vm = pl.BlockSpec(memory_space=pltpu.VMEM)
    n = len(parts)
    per = n // halves
    half = jax.ShapeDtypeStruct((per, *parts[0].shape), parts[0].dtype)
    return pl.pallas_call(
        functools.partial(kernel_stack, n, per),
        in_specs=[vm] * n,
        out_specs=[vm] * halves,
        out_shape=[half] * halves,
        compiler_params=params(8),
        name="stack",
    )(*parts)


def kernel_prep(s_ref, w_ref, wo_ref, at_ref, b_ref, sp_ref, spo_ref, out_ref):
    own = pl.multiple_of(s_ref[2] * 128, 128)
    other = pl.multiple_of(128 - s_ref[2] * 128, 128)
    b2 = jnp.concatenate([b_ref[:, pl.ds(own, 128)], b_ref[:, pl.ds(other, 128)]], axis=1)
    for r in range(0, out_ref.shape[0], BLK):
        rows = slice(r, r + BLK)
        ab = tn(at_ref[:, rows], b2)
        out_ref[rows, :128] = (w_ref[rows, :].astype(f32) + ab[:, :128]).astype(bf)
        out_ref[rows, 128:] = (wo_ref[rows, :].astype(f32) + ab[:, 128:]).astype(bf)
    for j in range(4):

        @pl.when(s_ref[7 + j] > 0)
        def _():
            sp = sp_ref[j] if j < 2 else spo_ref[j - 2]
            at = pl.ds(pl.multiple_of(s_ref[3 + j] * 128, 128), 128)
            cols = slice(0, 128) if j < 2 else slice(128, 256)
            out_ref[at, cols] = (out_ref[at, cols].astype(f32) + sp.astype(f32)).astype(bf)


def assemble(scr, ref_list, places, xi, zi, cols):
    for ref, place in zip(ref_list, places):
        for k, (dx, dz) in enumerate(place):
            row = (lax.rem(xi + dx + NX, NX) * NZ + lax.rem(zi + dz + NZ, NZ)) * 16
            scr[pl.ds(pl.multiple_of(row, 16), 16), :] = ref[k, :, cols]


def picks(base, r, s_ref, scr, cot_ref, gs_ref):
    for j in range(4):
        at = (s_ref[3 + j] - base) * 128 - r

        @pl.when((at >= 0) & (at < BLK))
        def _():
            c = s_ref[2] if j < 2 else 1 - s_ref[2]
            cot = cot_ref[:, pl.ds(pl.multiple_of(c * 128, 128), 128)]
            gs_ref[j] = tn(scr[:, pl.ds(pl.multiple_of(at, 128), 128)], cot)


def kernel_a(places, n, s_ref, *refs):
    chunks = refs[:n]
    w_ref, cot_ref, out_ref, ga_ref, clt_ref, low_ref, gs_ref, scr, ext = refs[n:]
    xi, zi = s_ref[0], s_ref[1]
    assemble(ext, chunks, places, xi, zi, slice(CA, CA + 128))
    low_ref[...] = ext[...]
    clt_ref[...] = ext[...].astype(f32).T.astype(bf)
    gs_ref[...] = jnp.zeros_like(gs_ref)
    for t, r in enumerate(range(0, CA, BLK)):
        buf = scr.at[t % 2]
        assemble(buf, chunks, places, xi, zi, slice(r, r + BLK))
        h = buf[...]
        part = jnp.dot(h, w_ref[r : r + BLK, :], preferred_element_type=f32)
        out_ref[...] = part if t == 0 else out_ref[...] + part
        ga_ref[:, r : r + BLK] = jnp.dot(clt_ref[:64, :], h, preferred_element_type=f32)
        picks(0, r, s_ref, buf, cot_ref, gs_ref)


def kernel_b(places, n, cb, s_ref, *refs):
    chunks = refs[:n]
    w_ref, cot_ref, outa_ref, clt_ref, low_ref, gsa_ref, send_ref, ga_ref, gs_ref, scr, acc = refs[n:]
    xi, zi, ci = s_ref[0], s_ref[1], s_ref[2]
    gs_ref[...] = gsa_ref[...]
    for t, r in enumerate(range(0, cb, BLK)):
        buf = scr.at[t % 2]
        assemble(buf, chunks, places, xi, zi, slice(r, r + BLK))
        h = buf[...]
        part = jnp.dot(h, w_ref[CA + r : CA + r + BLK, :], preferred_element_type=f32)
        acc[...] = (outa_ref[...] if t == 0 else acc[...]) + part
        ga_ref[:, r : r + BLK] = jnp.dot(clt_ref[:64, :], h, preferred_element_type=f32)
        picks(CA // 128, r, s_ref, buf, cot_ref, gs_ref)
    gb = tn(low_ref[...], cot_ref[...])[64:]
    for j in range(2):
        c = ci if j == 0 else 1 - ci
        for y in range(4):
            send_ref[c * 4 + y, :128, :] = acc[y * 128 : (y + 1) * 128, j * 128 : (j + 1) * 128].astype(bf)
            send_ref[j * 4 + y, 128:, :] = gb[:, j * 128 : (j + 1) * 128].astype(bf)


def kernel_final(got_ref, mixed_ref, gb_ref):
    acc = None
    for c in range(2):
        s = got_ref[c * 4].astype(f32)
        for y in range(1, 4):
            s = s + got_ref[c * 4 + y].astype(f32)
        for z in range(NZ):
            mixed_ref[z, c] = s[z * 16 : (z + 1) * 16].astype(bf)
        acc = s[128:] if acc is None else acc + s[128:]
    gb_ref[...] = acc


def kernel_add(x_ref, y_ref, o_ref):
    o_ref[...] = x_ref[...] + y_ref[...]


def kernel_add_to(_, x_ref, y_ref, o_ref):
    o_ref[...] = x_ref[...] + y_ref[...]


def params(mib=24):
    return pltpu.CompilerParams(vmem_limit_bytes=mib << 20)


def shards(gate, up, cot, w, a, b, sbv, rows, cols, counts):
    xi, zi, ci = lax.axis_index("x"), lax.axis_index("z"), lax.axis_index("c")
    chip = xi * NZ + zi
    K = w.shape[0]
    CB = K - CA
    first = ci == 0
    hid = (jax.nn.silu(gate.astype(f32)) * up.astype(f32)).astype(bf)
    own_b = hid[:, CA:]
    cl = lax.dot_general(cot, b, (((1,), (1,)), ((), ())), preferred_element_type=f32).astype(bf)
    lo = jnp.dot(hid, a, preferred_element_type=f32).astype(bf)
    own_a = jnp.concatenate([hid[:, :CA], cl, lo], axis=1)
    fb, bb = [own_b], [own_b]
    for _ in range(1, 4):
        fb.append(shift(fb[-1], "z", 1))
        bb.append(shift(bb[-1], "z", -1))
    sb = stack([own_b, fb[1], bb[1], fb[2], bb[2], fb[3], bb[3], shift(bb[3], "z", -1)], 2)
    sa = stack([own_a, shift(own_a, "x", 1), shift(own_a, "x", -1), shift(own_a, "x", 2)], 2)
    chunks_a, places_a = list(sa), [[(x, 0) for x in XS[:2]], [(x, 0) for x in XS[2:]]]
    f, r = list(sa), list(sa)
    for k in range(1, 5):
        for h in (0, 1):
            if k < 4 or h == 0:
                f[h] = shift(f[h], "z", 1)
                chunks_a.append(f[h])
                places_a.append([(x, -k) for x in XS[2 * h : 2 * h + 2]])
        for h in (1, 0):
            if k < 4 or h == 1:
                r[h] = shift(r[h], "z", -1)
                chunks_a.append(r[h])
                places_a.append([(x, k) for x in XS[2 * h : 2 * h + 2]])
    xf = [shift(sb[0], "x", 1), shift(sb[1], "x", 1)]
    xb = [shift(sb[0], "x", -1), shift(sb[1], "x", -1)]
    chunks_b = [*sb, *xf, *xb, shift(xf[0], "x", 1), shift(xb[1], "x", -1)]
    zs = [list(ZS[:4]), list(ZS[4:])]
    places_b = [[(x, z) for z in zs[h]] for x in XS for h in (0, 1)]
    sp = sbv[0, 0]
    w_o = shift(w, "c", 1)
    sp_o = shift(sp, "c", 1)
    b2 = lax.dynamic_slice_in_dim(b, chip * 256, 256, 1)
    r2 = lax.dynamic_slice_in_dim(rows[:, 0, :], chip * 2, 2, 0)
    live = jnp.arange(2, dtype=jnp.int32)[None, :] < lax.dynamic_slice_in_dim(counts[:, 0], chip * 2, 2, 0)[:, None]
    rel = jnp.where(first, r2, r2[::-1])
    rlive = jnp.where(first, live, live[::-1])
    scal = jnp.concatenate(
        [jnp.stack([xi, zi, ci]).astype(jnp.int32), rel.reshape(4), rlive.astype(jnp.int32).reshape(4)]
    )
    cc = lax.all_to_all(cot.reshape(16, 32, 256), ("x", "z"), split_axis=1, concat_axis=0)
    cc = cc.reshape(512, 256)

    vm = pl.BlockSpec(memory_space=pltpu.VMEM)
    sm = pl.BlockSpec(memory_space=pltpu.SMEM)
    cost = pl.CostEstimate(flops=2 * 512 * CA * 320, bytes_accessed=8 << 20, transcendentals=0)
    weff = pl.pallas_call(
        kernel_prep,
        in_specs=[sm] + [vm] * 6,
        out_specs=vm,
        out_shape=jax.ShapeDtypeStruct((K, 256), bf),
        compiler_params=params(GRANT),
        cost_estimate=pl.CostEstimate(flops=1 << 28, bytes_accessed=8 << 20, transcendentals=0),
        name="prep",
    )(scal, w, w_o, a.T, b2, sp, sp_o)
    na, nb = len(chunks_a), len(chunks_b)
    out_a, ga_a, clt, low, gs_a = pl.pallas_call(
        functools.partial(kernel_a, places_a, na),
        in_specs=[sm] + [vm] * (na + 2),
        out_specs=[vm] * 5,
        out_shape=[
            jax.ShapeDtypeStruct((512, 256), f32),
            jax.ShapeDtypeStruct((64, CA), f32),
            jax.ShapeDtypeStruct((128, 512), bf),
            jax.ShapeDtypeStruct((512, 128), bf),
            jax.ShapeDtypeStruct((4, 128, 128), f32),
        ],
        scratch_shapes=[pltpu.VMEM((2, 512, BLK), bf), pltpu.VMEM((512, 128), bf)],
        compiler_params=params(GRANT),
        cost_estimate=cost,
        name="colour_a",
    )(scal, *chunks_a, weff, cc)
    send, ga_b, gs = pl.pallas_call(
        functools.partial(kernel_b, places_b, nb, CB),
        in_specs=[sm] + [vm] * (nb + 6),
        out_specs=[vm] * 3,
        out_shape=[
            jax.ShapeDtypeStruct((8, 192, 128), bf),
            jax.ShapeDtypeStruct((64, CB), f32),
            jax.ShapeDtypeStruct((4, 128, 128), f32),
        ],
        scratch_shapes=[pltpu.VMEM((2, 512, BLK), bf), pltpu.VMEM((512, 256), f32)],
        compiler_params=params(GRANT),
        cost_estimate=cost,
        name="colour_b",
    )(scal, *chunks_b, weff, cc, out_a, clt, low, gs_a)
    got = lax.all_to_all(send, ("c", "y"), 0, 0, tiled=True)
    gsum = gs[:2] + shift(gs[2:], "c", 1)
    grad_blocks = jnp.where(rlive[0][:, None, None], gsum, 0.0)[None, None]
    left = pl.BlockSpec((64, CA // 2), lambda i: (0, i))
    ga_ao = shift(ga_a, "c", 1)
    ga_bo = shift(ga_b, "c", 1)
    grad_a = pl.pallas_call(
        kernel_add,
        grid=(2,),
        in_specs=[left, left],
        out_specs=left,
        out_shape=jax.ShapeDtypeStruct((64, K), f32),
        compiler_params=params(8),
        name="add_a",
    )(ga_a, ga_ao)
    grad_a = pl.pallas_call(
        kernel_add_to,
        grid=(2,),
        in_specs=[pl.BlockSpec(memory_space=pl.ANY), left, left],
        out_specs=pl.BlockSpec((64, CA // 2), lambda i: (0, i + 2)),
        out_shape=jax.ShapeDtypeStruct((64, K), f32),
        input_output_aliases={0: 0},
        compiler_params=params(8),
        name="add_b",
    )(grad_a, ga_b, ga_bo).T
    mixed, grad_b = pl.pallas_call(
        kernel_final,
        in_specs=[vm],
        out_specs=[vm, vm],
        out_shape=[jax.ShapeDtypeStruct((NZ, 2, 16, 128), bf), jax.ShapeDtypeStruct((64, 128), f32)],
        compiler_params=params(),
        name="final",
    )(got)
    return (mixed.reshape(256, 128), grad_a, grad_b, grad_blocks)


def solution(mesh):
    finer = Mesh(mesh.devices.reshape(4, 8, 2, 4), ("x", "z", "c", "y"))
    in_specs = (
        P(DP, "y"),
        P(DP, "y"),
        P(DP, None),
        P("y", DP),
        P("y", None),
        P(),
        P(DP, "y", None, None, None),
        P(None, "y", None),
        P(None, "y", None),
        P(None, "y"),
    )
    out_specs = (P("y", DP), P("y", None), P(None, DP), P(DP, "y", None, None, None))
    return jax.shard_map(shards, mesh=finer, in_specs=in_specs, out_specs=out_specs, check_vma=False)
```

```python
import functools

import jax
import jax.numpy as jnp
from jax import lax
from jax.experimental import pallas as pl
from jax.experimental.pallas import tpu as pltpu
from jax.sharding import Mesh
from jax.sharding import PartitionSpec as P


DP = ("x", "z", "c")
NX, NZ = 4, 8
bf = jnp.bfloat16
f32 = jnp.float32
CA = 3584
BLK = 1792
GRANT = 60
XS = (0, -1, 1, 2)
ZS = (0, -1, 1, -2, 2, -3, 3, 4)


def shift(a, axis, k):
    n = lax.axis_size(axis)
    return lax.ppermute(a, axis, [(i, (i + k) % n) for i in range(n)])


def tn(a, b):
    return lax.dot_general(a, b, (((0,), (0,)), ((), ())), preferred_element_type=f32)


def kernel_stack(n, per, *refs):
    for k in range(n):
        refs[n + k // per][k % per] = refs[k][...]


def stack(parts, halves):
    vm = pl.BlockSpec(memory_space=pltpu.VMEM)
    n = len(parts)
    per = n // halves
    half = jax.ShapeDtypeStruct((per, *parts[0].shape), parts[0].dtype)
    return pl.pallas_call(
        functools.partial(kernel_stack, n, per),
        in_specs=[vm] * n,
        out_specs=[vm] * halves,
        out_shape=[half] * halves,
        compiler_params=params(8),
        name="stack",
    )(*parts)


def kernel_prep(s_ref, w_ref, wo_ref, at_ref, b_ref, sp_ref, spo_ref, outa_ref, outb_ref, wv, wov, va, vb, sem):
    parts = ((va, outa_ref, 0), (vb, outb_ref, CA))

    def loads(t):
        rows = slice(parts[t][2], parts[t][2] + parts[t][0].shape[0])
        return (
            pltpu.make_async_copy(w_ref.at[rows, :], wv.at[rows, :], sem.at[0, t]),
            pltpu.make_async_copy(wo_ref.at[rows, :], wov.at[rows, :], sem.at[1, t]),
        )

    def store(t):
        return pltpu.make_async_copy(parts[t][0], parts[t][1], sem.at[2, t])

    for t in range(2):
        for copy in loads(t):
            copy.start()
    own = pl.multiple_of(s_ref[2] * 128, 128)
    other = pl.multiple_of(128 - s_ref[2] * 128, 128)
    b2 = jnp.concatenate([b_ref[:, pl.ds(own, 128)], b_ref[:, pl.ds(other, 128)]], axis=1)
    for t, (out_ref, _, base) in enumerate(parts):
        for copy in loads(t):
            copy.wait()
        for r in range(0, out_ref.shape[0], BLK):
            rows = slice(base + r, base + r + BLK)
            ab = tn(at_ref[:, rows], b2)
            out_ref[r : r + BLK, :128] = (wv[rows, :].astype(f32) + ab[:, :128]).astype(bf)
            out_ref[r : r + BLK, 128:] = (wov[rows, :].astype(f32) + ab[:, 128:]).astype(bf)
        for j in range(4):
            at = s_ref[3 + j] * 128 - base

            @pl.when((at >= 0) & (at < out_ref.shape[0]) & (s_ref[7 + j] > 0))
            def _():
                sp = sp_ref[j] if j < 2 else spo_ref[j - 2]
                rows = pl.ds(pl.multiple_of(at, 128), 128)
                cols = slice(0, 128) if j < 2 else slice(128, 256)
                out_ref[rows, cols] = (out_ref[rows, cols].astype(f32) + sp.astype(f32)).astype(bf)

        store(t).start()
    for t in range(2):
        store(t).wait()


def fetch(scr, ref_list, places, xi, zi, cols, sem):
    for ref, place in zip(ref_list, places):
        for k, (dx, dz) in enumerate(place):
            row = (lax.rem(xi + dx + NX, NX) * NZ + lax.rem(zi + dz + NZ, NZ)) * 16
            here = scr.at[pl.ds(pl.multiple_of(row, 16), 16), :]
            pltpu.make_async_copy(ref.at[k, :, cols], here, sem).start()


def arrived(scr, sem):
    pltpu.make_async_copy(scr, scr, sem).wait()


def picks(base, r, s_ref, scr, cot_ref, gs_ref):
    for j in range(4):
        at = (s_ref[3 + j] - base) * 128 - r

        @pl.when((at >= 0) & (at < BLK))
        def _():
            c = s_ref[2] if j < 2 else 1 - s_ref[2]
            cot = cot_ref[:, pl.ds(pl.multiple_of(c * 128, 128), 128)]
            gs_ref[j] = tn(scr[:, pl.ds(pl.multiple_of(at, 128), 128)], cot)


def kernel_main(places_a, na, places_b, nb, s_ref, *refs):
    ca, cb = refs[:na], refs[na : na + nb]
    wa_ref, wb_ref, cot_ref, send_ref, ga_ref, gs_ref, scr, wv, ext, clt, acc, sem = refs[na + nb :]
    xi, zi, ci = s_ref[0], s_ref[1], s_ref[2]
    load_a = pltpu.make_async_copy(wa_ref, wv.at[:CA, :], sem.at[5])
    load_b = pltpu.make_async_copy(wb_ref, wv.at[CA:, :], sem.at[6])
    fetch(ext, ca, places_a, xi, zi, slice(CA, CA + 128), sem.at[0])
    fetch(scr.at[0], ca, places_a, xi, zi, slice(0, BLK), sem.at[1])
    load_a.start()
    fetch(scr.at[1], ca, places_a, xi, zi, slice(BLK, 2 * BLK), sem.at[2])
    fetch(scr.at[2], cb, places_b, xi, zi, slice(0, BLK), sem.at[3])
    load_b.start()
    fetch(scr.at[3], cb, places_b, xi, zi, slice(BLK, 2 * BLK), sem.at[4])
    arrived(ext, sem.at[0])
    clt[...] = ext[...].astype(f32).T.astype(bf)
    gb = tn(ext[...], cot_ref[...])[64:]
    for j in range(2):
        for y in range(4):
            send_ref[j * 4 + y, 128:, :] = gb[:, j * 128 : (j + 1) * 128].astype(bf)
    for t in range(4):
        r = t * BLK
        buf = scr.at[t]
        arrived(buf, sem.at[1 + t])
        if t == 0:
            load_a.wait()
        if t == 2:
            load_b.wait()
        h = buf[...]
        part = jnp.dot(h, wv[r : r + BLK, :], preferred_element_type=f32)
        acc[...] = part if t == 0 else acc[...] + part
        ga_ref[:, r : r + BLK] = jnp.dot(clt[:64, :], h, preferred_element_type=f32)
        picks(0, r, s_ref, buf, cot_ref, gs_ref)
    for j in range(2):
        c = ci if j == 0 else 1 - ci
        for y in range(4):
            send_ref[c * 4 + y, :128, :] = acc[y * 128 : (y + 1) * 128, j * 128 : (j + 1) * 128].astype(bf)


def kernel_final(got_ref, mixed_ref, gb_ref):
    acc = None
    for c in range(2):
        s = got_ref[c * 4].astype(f32)
        for y in range(1, 4):
            s = s + got_ref[c * 4 + y].astype(f32)
        for z in range(NZ):
            mixed_ref[z, c] = s[z * 16 : (z + 1) * 16].astype(bf)
        acc = s[128:] if acc is None else acc + s[128:]
    gb_ref[...] = acc


def kernel_add(x_ref, y_ref, o_ref):
    o_ref[...] = x_ref[...] + y_ref[...]


def params(mib=24):
    return pltpu.CompilerParams(vmem_limit_bytes=mib << 20)


def shards(gate, up, cot, w, a, b, sbv, rows, cols, counts):
    xi, zi, ci = lax.axis_index("x"), lax.axis_index("z"), lax.axis_index("c")
    chip = xi * NZ + zi
    K = w.shape[0]
    CB = K - CA
    first = ci == 0
    hid = (jax.nn.silu(gate.astype(f32)) * up.astype(f32)).astype(bf)
    own_b = hid[:, CA:]
    cl = lax.dot_general(cot, b, (((1,), (1,)), ((), ())), preferred_element_type=f32).astype(bf)
    lo = jnp.dot(hid, a, preferred_element_type=f32).astype(bf)
    own_a = jnp.concatenate([hid[:, :CA], cl, lo], axis=1)
    fb, bb = [own_b], [own_b]
    for _ in range(1, 4):
        fb.append(shift(fb[-1], "z", 1))
        bb.append(shift(bb[-1], "z", -1))
    sb = stack([own_b, fb[1], bb[1], fb[2], bb[2], fb[3], bb[3], shift(bb[3], "z", -1)], 2)
    sa = stack([own_a, shift(own_a, "x", 1), shift(own_a, "x", -1), shift(own_a, "x", 2)], 2)
    chunks_a, places_a = list(sa), [[(x, 0) for x in XS[:2]], [(x, 0) for x in XS[2:]]]
    f, r = list(sa), list(sa)
    for k in range(1, 5):
        for h in (0, 1):
            if k < 4 or h == 0:
                f[h] = shift(f[h], "z", 1)
                chunks_a.append(f[h])
                places_a.append([(x, -k) for x in XS[2 * h : 2 * h + 2]])
        for h in (1, 0):
            if k < 4 or h == 1:
                r[h] = shift(r[h], "z", -1)
                chunks_a.append(r[h])
                places_a.append([(x, k) for x in XS[2 * h : 2 * h + 2]])
    xf = [shift(sb[0], "x", 1), shift(sb[1], "x", 1)]
    xb = [shift(sb[0], "x", -1), shift(sb[1], "x", -1)]
    chunks_b = [*sb, *xf, *xb, shift(xf[0], "x", 1), shift(xb[1], "x", -1)]
    zs = [list(ZS[:4]), list(ZS[4:])]
    places_b = [[(x, z) for z in zs[h]] for x in XS for h in (0, 1)]
    sp = sbv[0, 0]
    w_o = shift(w, "c", 1)
    sp_o = shift(sp, "c", 1)
    b2 = lax.dynamic_slice_in_dim(b, chip * 256, 256, 1)
    r2 = lax.dynamic_slice_in_dim(rows[:, 0, :], chip * 2, 2, 0)
    live = jnp.arange(2, dtype=jnp.int32)[None, :] < lax.dynamic_slice_in_dim(counts[:, 0], chip * 2, 2, 0)[:, None]
    rel = jnp.where(first, r2, r2[::-1])
    rlive = jnp.where(first, live, live[::-1])
    scal = jnp.concatenate(
        [jnp.stack([xi, zi, ci]).astype(jnp.int32), rel.reshape(4), rlive.astype(jnp.int32).reshape(4)]
    )
    cc = lax.all_to_all(cot.reshape(16, 32, 256), ("x", "z"), split_axis=1, concat_axis=0)
    cc = cc.reshape(512, 256)

    vm = pl.BlockSpec(memory_space=pltpu.VMEM)
    sm = pl.BlockSpec(memory_space=pltpu.SMEM)
    anyw = pl.BlockSpec(memory_space=pl.ANY)
    cost = pl.CostEstimate(flops=2 * 512 * CA * 320, bytes_accessed=8 << 20, transcendentals=0)
    weff_a, weff_b = pl.pallas_call(
        kernel_prep,
        in_specs=[sm] + [anyw] * 2 + [vm] * 4,
        out_specs=[anyw] * 2,
        out_shape=[jax.ShapeDtypeStruct((CA, 256), bf), jax.ShapeDtypeStruct((CB, 256), bf)],
        scratch_shapes=[pltpu.VMEM((K, 128), bf)] * 2
        + [pltpu.VMEM((CA, 256), bf), pltpu.VMEM((CB, 256), bf), pltpu.SemaphoreType.DMA((3, 2))],
        compiler_params=params(GRANT),
        cost_estimate=pl.CostEstimate(flops=1 << 28, bytes_accessed=8 << 20, transcendentals=0),
        name="prep",
    )(scal, w, w_o, a.T, b2, sp, sp_o)
    na, nb = len(chunks_a), len(chunks_b)
    send, ga, gs = pl.pallas_call(
        functools.partial(kernel_main, places_a, na, places_b, nb),
        in_specs=[sm] + [anyw] * (na + nb + 2) + [vm],
        out_specs=[vm] * 3,
        out_shape=[
            jax.ShapeDtypeStruct((8, 192, 128), bf),
            jax.ShapeDtypeStruct((64, K), f32),
            jax.ShapeDtypeStruct((4, 128, 128), f32),
        ],
        scratch_shapes=[
            pltpu.VMEM((4, 512, BLK), bf),
            pltpu.VMEM((K, 256), bf),
            pltpu.VMEM((512, 128), bf),
            pltpu.VMEM((128, 512), bf),
            pltpu.VMEM((512, 256), f32),
            pltpu.SemaphoreType.DMA((7,)),
        ],
        compiler_params=params(GRANT),
        cost_estimate=cost,
        name="main",
    )(scal, *chunks_a, *chunks_b, weff_a, weff_b, cc)
    got = lax.all_to_all(send, ("c", "y"), 0, 0, tiled=True)
    gsum = gs[:2] + shift(gs[2:], "c", 1)
    grad_blocks = jnp.where(rlive[0][:, None, None], gsum, 0.0)[None, None]
    left = pl.BlockSpec((64, CA // 2), lambda i: (0, i))
    ga_o = shift(ga, "c", 1)
    grad_a = pl.pallas_call(
        kernel_add,
        grid=(4,),
        in_specs=[left, left],
        out_specs=left,
        out_shape=jax.ShapeDtypeStruct((64, K), f32),
        compiler_params=params(8),
        name="add_a",
    )(ga, ga_o).T
    mixed, grad_b = pl.pallas_call(
        kernel_final,
        in_specs=[vm],
        out_specs=[vm, vm],
        out_shape=[jax.ShapeDtypeStruct((NZ, 2, 16, 128), bf), jax.ShapeDtypeStruct((64, 128), f32)],
        compiler_params=params(),
        name="final",
    )(got)
    return (mixed.reshape(256, 128), grad_a, grad_b, grad_blocks)


def solution(mesh):
    finer = Mesh(mesh.devices.reshape(4, 8, 2, 4), ("x", "z", "c", "y"))
    in_specs = (
        P(DP, "y"),
        P(DP, "y"),
        P(DP, None),
        P("y", DP),
        P("y", None),
        P(),
        P(DP, "y", None, None, None),
        P(None, "y", None),
        P(None, "y", None),
        P(None, "y"),
    )
    out_specs = (P("y", DP), P("y", None), P(None, DP), P(DP, "y", None, None, None))
    return jax.shard_map(shards, mesh=finer, in_specs=in_specs, out_specs=out_specs, check_vma=False)
```
